32 devices in a mesh: groups: 2 (over x), mset: 16 (over z, y, core).
Axes of the slice: x: 2, y: 2, z: 4, core: 2. Of those that a mesh axis runs over, the one named last changes fastest.
Arguments:
- m_list: int32 [16], replicated, may hold values from 1536 to 3071, as said below
- coeff: bfloat16 [32, 32, 1536], P(('groups', 'mset')), parts along dimension 0, may hold values from -6 to 6
- blocks: bfloat16 [32, 1536, 1536], P(('groups', 'mset')), parts along dimension 0, may hold values from -0.15625 to 0.15625
- legendre: bfloat16 [512, 16, 1536], P(('groups', 'mset')), parts along dimension 0, may hold values from -0.15625 to 0.15625
Outputs:
- sky_map: bfloat16 [512, 16, 8192], P(('groups', 'mset')), parts along dimension 0
The draws below stay inside these ranges and needn't reach their ends.
There are 2 independent parts, one for each index of `groups`. The reference program is written for one: setup_inputs(seed, part) draws one part's arguments, and reference() takes and returns one part's arrays. A program takes and returns all parts, laid end to end along the dimension named above; an argument that names none is the same for every part. Nothing has to cross between parts.
Inputs may be any that keep to these rules, and one draw needn't show every extreme that they name: `m_list`: 16 distinct values; the value 3072 - 1536, a block of full order 1536, is always among them.
All inputs are finite; a program needn't handle non-finite values.
Results may differ from the reference program's by a relative error of at most 0.0062.
Values may be sent and summed in bfloat16 or wider, within the bound.
A program may use at most 64 MiB of HBM per device.

```python
import math
import jax
import jax.numpy as jnp
from jax import lax

LL = 3072
LB = 1536
REAL = 16
COLS = 32
NPHI = 8192
M_SUB = 16
CYCLES = 256


def draw_m_list(key, part):
    shuffled = jax.random.permutation(jax.random.fold_in(key, 11), LB).astype(jnp.int32)
    target = jax.random.randint(jax.random.fold_in(key, 12), (), 0, M_SUB).astype(jnp.int32)
    zero_pos = jnp.argmax(shuffled == 0).astype(jnp.int32)
    moved_value = shuffled[target]
    shuffled = shuffled.at[zero_pos].set(moved_value)
    shuffled = shuffled.at[target].set(jnp.int32(0))
    return (LL - LB + shuffled[:M_SUB]).astype(jnp.int32)


def shard_levels(rng, shape, shards, least, high):
    def one(dim, parts):
        heights = jax.random.uniform(jax.random.fold_in(jax.random.fold_in(rng, 6), dim), (parts,), jnp.float32, least / len(shards), high / len(shards))
        return jnp.repeat(jnp.exp(heights), shape[dim] // parts).reshape((-1,) + (1,) * (len(shape) - dim - 1))

    level = one(*shards[0])
    for cut in shards[1:]:
        level = level * one(*cut)
    return level


def scatter_about(own_key, dims, scale, bound, pieces=(), kind=jnp.bfloat16):
    gain = shard_levels(own_key, dims, pieces, -0.22, 0.18) if pieces else 1.0
    array = jax.random.normal(own_key, dims, jnp.float32) * scale * gain
    return jnp.minimum(jnp.maximum(array, -bound), bound).astype(kind)


def setup_inputs(seed: int = 0, part: int = 0) -> dict:
    arg_keys = jax.random.split(jax.random.key(seed), 5)
    part_keys = jax.random.split(jax.random.fold_in(arg_keys[4], part), 5)
    return {
        "m_list": draw_m_list(jax.random.fold_in(arg_keys[4], 71), part),
        "coeff": scatter_about(part_keys[1], (M_SUB, COLS, LB), 1.0, 6.0, ((0, 16),)),
        "blocks": scatter_about(part_keys[2], (M_SUB, LB, LB), LB ** -0.5, 0.15625, ((0, 16),)),
        "legendre": scatter_about(part_keys[3], (CYCLES, M_SUB, LB), LB ** -0.5, 0.15625, ((0, 16),)),
    }


def fourier_table(m_values, pixels):
    pixel_index = jnp.arange(pixels, dtype=jnp.int32)
    phases = m_values.astype(jnp.int32)[:, None] * pixel_index[None, :] % pixels
    angles = phases.astype(jnp.float32) * (2.0 * math.pi / pixels)
    cos_part = jnp.cos(angles).astype(jnp.bfloat16)
    sin_part = jnp.sin(angles).astype(jnp.bfloat16)
    return jnp.concatenate([cos_part, -sin_part], axis=0)

def reference(m_list, coeff, blocks, legendre):
    orders = (LL - m_list).astype(jnp.int32)
    valid_mask = jnp.arange(LB, dtype=jnp.int32)[None, :] < orders[:, None]

    def block_apply(items):
        column_block, inverse, valid_row = items
        masked = jnp.where(valid_row[None, :], column_block, jnp.zeros_like(column_block))
        products = jnp.dot(masked.astype(jnp.float32), inverse.astype(jnp.float32), preferred_element_type=jnp.float32)
        return jnp.where(valid_row[None, :], products, jnp.zeros_like(products)).astype(jnp.bfloat16)
    filtered = lax.map(block_apply, (coeff, blocks, valid_mask))
    filtered_wide = filtered.astype(jnp.float32)

    def cycle_sum(cycle_table):
        return jnp.einsum('mj,mcj->mc', cycle_table.astype(jnp.float32), filtered_wide).astype(jnp.bfloat16)
    harmonics = lax.map(cycle_sum, legendre)
    real_part = harmonics[:, :, :REAL]
    imag_part = harmonics[:, :, REAL:]
    stacked = jnp.concatenate([real_part, imag_part], axis=1)
    flattened = jnp.transpose(stacked, (0, 2, 1)).reshape(CYCLES * REAL, 2 * M_SUB)
    trig_table = fourier_table(m_list, NPHI)
    summed = jnp.dot(flattened.astype(jnp.float32), trig_table.astype(jnp.float32), preferred_element_type=jnp.float32)
    scaled = summed * (1.0 / math.sqrt(M_SUB))
    return scaled.astype(jnp.bfloat16).reshape(CYCLES, REAL, NPHI)
```

```python
import functools
import math

import jax
import jax.numpy as jnp
from jax import lax
from jax.experimental import pallas as pl
from jax.experimental.pallas import tpu as pltpu
from jax.sharding import PartitionSpec as P

LL = 3072
REAL = 16
NPHI = 8192
LANES = 128
MESH = pl.DeviceIdType.MESH
F32 = jnp.float32
BF16 = jnp.bfloat16


def iota(shape, dim):
    return lax.broadcasted_iota(jnp.int32, shape, dim)


def split_index(x, size):
    if size & (size - 1) == 0:
        shift = size.bit_length() - 1
        return lax.shift_right_logical(x, jnp.int32(shift)), lax.bitwise_and(x, jnp.int32(size - 1))
    quotient = x // size
    return quotient, x - quotient * size


def harmonics_kernel(
    n, chunks, m_ref, coeff_ref, blocks_ref, leg_ref, out_ref, table_ref,
    coeff_v, blocks_v, leg_v, gathered, expand, acc,
    load_sem, recv_sem, up_sem, down_sem, side_sem, sib_sem,
):
    subset = m_ref.shape[0]
    cols, order_max = coeff_ref.shape[1], coeff_ref.shape[2]
    width = order_max // chunks
    group = 4
    depth = n // group
    rows_in = leg_ref.shape[0]
    rows_out = out_ref.shape[0]
    cycles = rows_in // subset
    me = lax.axis_index("mset")
    core = lax.rem(me, 2)
    side = lax.rem(lax.div(me, 2), 2)
    z = lax.div(me, group)
    sibling = me + 1 - 2 * core
    partner = me + 2 - 4 * side

    def load_block(q):
        return pltpu.make_async_copy(
            blocks_ref.at[0, :, pl.ds(q * width, width)], blocks_v.at[q], load_sem.at[q]
        )

    coeff_load = pltpu.make_async_copy(coeff_ref.at[0], coeff_v, load_sem.at[chunks])
    leg_load = pltpu.make_async_copy(leg_ref, leg_v, load_sem.at[chunks + 1])
    coeff_load.start()
    for q in range(chunks):
        load_block(q).start()
    leg_load.start()

    barrier = pltpu.get_barrier_semaphore()

    def greet(target):
        pl.semaphore_signal(barrier, inc=1, device_id={"mset": target}, device_id_type=MESH)

    greet(sibling)
    greet(partner)

    @pl.when(z > 0)
    def _():
        greet(me - group)

    @pl.when(z < depth - 1)
    def _():
        greet(me + group)

    def piece(src, q):
        return gathered.at[src, :, pl.ds(q * width, width)]

    def copy(src, q, target, send_sem):
        return pltpu.make_async_remote_copy(
            src_ref=piece(src, q),
            dst_ref=piece(src, q),
            send_sem=send_sem,
            recv_sem=recv_sem.at[q, src],
            device_id={"mset": target},
            device_id_type=MESH,
        )

    def to_up(src, q):
        return copy(src, q, me + group, up_sem.at[q, lax.div(src, group)])

    def to_down(src, q):
        return copy(src, q, me - group, down_sem.at[q, lax.div(src, group)])

    def to_side(src, q):
        return copy(src, q, partner, side_sem.at[q, lax.div(src, group)])

    def to_sib(src, q):
        return copy(src, q, sibling, sib_sem.at[q, lax.div(src, 2)])

    def arrive(src, q):
        copy(src, q, sibling, sib_sem.at[q, lax.div(src, 2)]).wait_recv()

    order = LL - m_ref[me]
    coeff_load.wait()
    masked = jnp.where(iota((cols, order_max), 1) < order, coeff_v[...].astype(F32), 0.0).astype(BF16)
    for q in range(chunks):
        load_block(q).wait()
        product = jnp.dot(masked, blocks_v[q], preferred_element_type=F32)
        valid = iota((cols, width), 1) + q * width < order
        gathered[me, :, pl.ds(q * width, width)] = jnp.where(valid, product, 0.0).astype(BF16)
        if q == 0:
            peers = 2 + jnp.where(z > 0, 1, 0) + jnp.where(z < depth - 1, 1, 0)
            pl.semaphore_wait(barrier, peers)

        to_side(me, q).start()

        @pl.when(z < depth - 1)
        def _():
            to_up(me, q).start()

        @pl.when(z > 0)
        def _():
            to_down(me, q).start()

        to_sib(me, q).start()

    m_col = jnp.zeros((subset, LANES), jnp.int32)
    slot = iota((subset, LANES), 0)
    for i in range(subset):
        m_col = jnp.where(slot == i, m_ref[i], m_col)
    lane = iota((subset, LANES), 1)
    fine = split_index(m_col * lane, NPHI)[1].astype(F32) * (2.0 * math.pi / NPHI)
    coarse = split_index(m_col * (lane * LANES), NPHI)[1].astype(F32) * (2.0 * math.pi / NPHI)
    fine_cos, fine_sin = jnp.cos(fine), jnp.sin(fine)
    coarse_cos, coarse_sin = jnp.cos(coarse), jnp.sin(coarse)
    for a in range(NPHI // LANES):
        c = coarse_cos[:, a : a + 1]
        s = coarse_sin[:, a : a + 1]
        table_ref[0:subset, a * LANES : (a + 1) * LANES] = (c * fine_cos - s * fine_sin).astype(BF16)
        table_ref[subset : 2 * subset, a * LANES : (a + 1) * LANES] = (
            -(s * fine_cos + c * fine_sin)
        ).astype(BF16)

    out_cycle = split_index(iota((rows_out, rows_in), 0), REAL)[0]
    in_cycle = split_index(iota((rows_out, rows_in), 1), subset)[0]
    expand[...] = jnp.where(out_cycle == in_cycle, 1.0, 0.0).astype(BF16)
    acc[...] = jnp.zeros_like(acc)
    leg_load.wait()

    span = group * cols

    def absorb(zz):
        values = gathered[pl.ds(zz * group, group)].reshape(span, order_max)
        cross = lax.dot_general(
            leg_v[...], values, (((1,), (1,)), ((), ())), preferred_element_type=F32
        )
        row_m = split_index(iota((rows_in, span), 0), subset)[1]
        col_m = split_index(iota((rows_in, span), 1), cols)[0] + zz * group
        own = jnp.where(row_m == col_m, cross, 0.0).astype(BF16)
        spread = jnp.dot(expand[...], own, preferred_element_type=F32)
        row_s = split_index(iota((rows_out, span), 0), REAL)[1]
        col_s = split_index(iota((rows_out, span), 1), REAL)[1]
        picked = jnp.where(row_s == col_s, spread, 0.0).astype(BF16)
        src = iota((span, 2 * subset), 0)
        src_m, src_c = split_index(src, cols)
        dst_part, dst_m = split_index(iota((span, 2 * subset), 1), subset)
        hit = (src_m + zz * group == dst_m) & (split_index(src_c, REAL)[0] == dst_part)
        select = jnp.where(hit, 1.0, 0.0).astype(BF16)
        acc[...] += jnp.dot(picked, select, preferred_element_type=F32)

    def row(zz):
        return zz * group + side * 2 + core, zz * group + (1 - side) * 2 + core

    def finish(zz):
        for s in range(2):
            for q in range(chunks):
                arrive(zz * group + s * 2 + 1 - core, q)
        absorb(zz)

    def relay_line(zz, forward):
        mine, _ = row(zz)
        for q in range(chunks):
            arrive(mine, q)
            forward(mine, q)
            to_side(mine, q).start()
            to_sib(mine, q).start()

    def relay_side(zz):
        _, other = row(zz)
        for q in range(chunks):
            arrive(other, q)
            to_sib(other, q).start()

    def below(d):
        def forward(src, q):
            @pl.when(z < depth - 1)
            def _():
                to_up(src, q).start()

        relay_line(z - d, forward)

    def above(d):
        def forward(src, q):
            @pl.when(z > 0)
            def _():
                to_down(src, q).start()

        relay_line(z + d, forward)

    if depth > 1:
        pl.when(z >= 1)(lambda: below(1))
        pl.when(z <= depth - 2)(lambda: above(1))
    relay_side(z)
    finish(z)
    for d in range(1, depth):
        if d + 1 < depth:
            pl.when(z >= d + 1)(functools.partial(below, d + 1))
            pl.when(z <= depth - 2 - d)(functools.partial(above, d + 1))
        pl.when(z >= d)(functools.partial(lambda d: relay_side(z - d), d))
        pl.when(z <= depth - 1 - d)(functools.partial(lambda d: relay_side(z + d), d))
        pl.when(z >= d)(functools.partial(lambda d: finish(z - d), d))
        pl.when(z <= depth - 1 - d)(functools.partial(lambda d: finish(z + d), d))

    out_ref[...] = acc[...].astype(BF16)

    for zz in range(depth):
        mine, other = row(zz)
        for q in range(chunks):
            to_side(mine, q).wait_send()
            to_sib(mine, q).wait_send()
            to_sib(other, q).wait_send()

            @pl.when((z < depth - 1) & (zz <= z))
            def _():
                to_up(mine, q).wait_send()

            @pl.when((z > 0) & (zz >= z))
            def _():
                to_down(mine, q).wait_send()


def synthesis_kernel(tiles, scale, h_ref, table_ref, out_ref, buf, sem):
    tile = out_ref.shape[1] // tiles
    copies = []
    for t in range(tiles):
        cut = slice(t * tile, (t + 1) * tile)
        total = jnp.dot(h_ref[...], table_ref[:, cut], preferred_element_type=F32)
        buf[:, cut] = (total * scale).astype(BF16)
        copies.append(pltpu.make_async_copy(buf.at[:, cut], out_ref.at[:, cut], sem.at[t]))
        copies[-1].start()
    for c in copies:
        c.wait()


def body(n, m_list, coeff, blocks, legendre):
    per_device, cols, order_max = coeff.shape
    assert per_device == 1 and n % 4 == 0
    cycles, subset, _ = legendre.shape
    chunks = 3
    depth = n // 4
    rows_in, rows_out = cycles * subset, cycles * REAL
    vmem = pl.BlockSpec(memory_space=pltpu.VMEM)
    hbm = pl.BlockSpec(memory_space=pl.ANY)
    dma = pltpu.SemaphoreType.DMA
    harmonics, table = pl.pallas_call(
        functools.partial(harmonics_kernel, n, chunks),
        out_shape=(
            jax.ShapeDtypeStruct((rows_out, 2 * subset), BF16),
            jax.ShapeDtypeStruct((2 * subset, NPHI), BF16),
        ),
        in_specs=[pl.BlockSpec(memory_space=pltpu.SMEM), hbm, hbm, hbm],
        out_specs=(vmem, vmem),
        scratch_shapes=[
            pltpu.VMEM((cols, order_max), BF16),
            pltpu.VMEM((chunks, order_max, order_max // chunks), BF16),
            pltpu.VMEM((rows_in, order_max), BF16),
            pltpu.VMEM((n, cols, order_max), BF16),
            pltpu.VMEM((rows_out, rows_in), BF16),
            pltpu.VMEM((rows_out, 2 * subset), F32),
            dma((chunks + 2,)),
            dma((chunks, n)),
            dma((chunks, depth)),
            dma((chunks, depth)),
            dma((chunks, depth)),
            dma((chunks, 2 * depth)),
        ],
        compiler_params=pltpu.CompilerParams(collective_id=0, has_side_effects=True),
        name="harmonics",
    )(m_list, coeff, blocks, legendre.reshape(rows_in, order_max))
    tiles = 8
    sky = pl.pallas_call(
        functools.partial(synthesis_kernel, tiles, 1.0 / math.sqrt(subset)),
        out_shape=jax.ShapeDtypeStruct((rows_out, NPHI), BF16),
        in_specs=[vmem, vmem],
        out_specs=hbm,
        scratch_shapes=[pltpu.VMEM((rows_out, NPHI), BF16), dma((tiles,))],
        name="synthesis",
    )(harmonics, table)
    return sky.reshape(cycles, REAL, NPHI)


def solution(mesh):
    spec = P(("groups", "mset"), None, None)
    return jax.shard_map(
        functools.partial(body, mesh.shape["mset"]),
        mesh=mesh,
        in_specs=(P(), spec, spec, spec),
        out_specs=spec,
        check_vma=False,
    )
```

```python
import functools
import math

import jax
import jax.numpy as jnp
from jax import lax
from jax.experimental import pallas as pl
from jax.experimental.pallas import tpu as pltpu
from jax.sharding import PartitionSpec as P

LL = 3072
REAL = 16
NPHI = 8192
LANES = 128
MESH = pl.DeviceIdType.MESH
F32 = jnp.float32
BF16 = jnp.bfloat16


def iota(shape, dim):
    return lax.broadcasted_iota(jnp.int32, shape, dim)


def split_index(x, size):
    if size & (size - 1) == 0:
        shift = size.bit_length() - 1
        return lax.shift_right_logical(x, jnp.int32(shift)), lax.bitwise_and(x, jnp.int32(size - 1))
    quotient = x // size
    return quotient, x - quotient * size


def harmonics_kernel(
    n, chunks, m_ref, coeff_ref, blocks_ref, leg_ref, out_ref,
    coeff_v, blocks_v, leg_v, leg_away, leg_here, gathered, harm_away, harm,
    load_sem, recv_sem, up_sem, down_sem, sib_sem, leg_send, leg_recv, harm_sem,
):
    subset = m_ref.shape[0]
    cols, order_max = coeff_ref.shape[1], coeff_ref.shape[2]
    width = order_max // chunks
    group = 4
    depth = n // group
    line = 2 * depth
    rows_in = leg_ref.shape[0]
    rows_out = out_ref.shape[0]
    cycles = rows_in // subset
    rows_half = cycles * line
    span = line * cols
    me = lax.axis_index("mset")
    core = lax.rem(me, 2)
    side = lax.rem(lax.div(me, 2), 2)
    z = lax.div(me, group)
    sibling = me + 1 - 2 * core
    partner = me + 2 - 4 * side

    def load_block(q):
        return pltpu.make_async_copy(
            blocks_ref.at[0, :, pl.ds(q * width, width)], blocks_v.at[q], load_sem.at[q]
        )

    coeff_load = pltpu.make_async_copy(coeff_ref.at[0], coeff_v, load_sem.at[chunks])
    leg_load = pltpu.make_async_copy(leg_ref, leg_v, load_sem.at[chunks + 1])
    coeff_load.start()
    for q in range(chunks):
        load_block(q).start()
    leg_load.start()

    barrier = pltpu.get_barrier_semaphore()

    def greet(target):
        pl.semaphore_signal(barrier, inc=1, device_id={"mset": target}, device_id_type=MESH)

    greet(sibling)
    greet(partner)

    @pl.when(z > 0)
    def _():
        greet(me - group)

    @pl.when(z < depth - 1)
    def _():
        greet(me + group)

    def piece(pos, q):
        return gathered.at[q, pos]

    def copy(pos, q, target, send_sem):
        return pltpu.make_async_remote_copy(
            src_ref=piece(pos, q),
            dst_ref=piece(pos, q),
            send_sem=send_sem,
            recv_sem=recv_sem.at[q, pos],
            device_id={"mset": target},
            device_id_type=MESH,
        )

    def to_up(zz, q):
        return copy(2 * zz + core, q, me + group, up_sem.at[q, zz])

    def to_down(zz, q):
        return copy(2 * zz + core, q, me - group, down_sem.at[q, zz])

    def to_sib(zz, q):
        return copy(2 * zz + core, q, sibling, sib_sem.at[q, zz])

    def arrive(pos, q):
        copy(pos, q, sibling, sib_sem.at[q, 0]).wait_recv()

    def leg_copy(q):
        return pltpu.make_async_remote_copy(
            src_ref=leg_away.at[:, pl.ds(q * width, width)],
            dst_ref=leg_here.at[1, :, pl.ds(q * width, width)],
            send_sem=leg_send.at[q],
            recv_sem=leg_recv.at[q],
            device_id={"mset": partner},
            device_id_type=MESH,
        )

    def side_rows(which):
        row_cycle, row_pos = split_index(iota((rows_half, rows_in), 0), line)
        row_zz, row_core = split_index(row_pos, 2)
        wanted = row_cycle * subset + row_zz * group + which * 2 + row_core
        return jnp.where(iota((rows_half, rows_in), 1) == wanted, 1.0, 0.0).astype(BF16)

    order = LL - m_ref[me]
    coeff_load.wait()
    masked = jnp.where(iota((cols, order_max), 1) < order, coeff_v[...].astype(F32), 0.0).astype(BF16)
    for q in range(chunks):
        load_block(q).wait()
        product = jnp.dot(masked, blocks_v[q], preferred_element_type=F32)
        valid = iota((cols, width), 1) + q * width < order
        gathered[q, 2 * z + core] = jnp.where(valid, product, 0.0).astype(BF16)

        if q == 0:
            peers = 2 + jnp.where(z > 0, 1, 0) + jnp.where(z < depth - 1, 1, 0)
            pl.semaphore_wait(barrier, peers)

        @pl.when(z < depth - 1)
        def _():
            to_up(z, q).start()

        @pl.when(z > 0)
        def _():
            to_down(z, q).start()

        to_sib(z, q).start()

    away = side_rows(1 - side)
    leg_load.wait()
    for q in range(chunks):
        cut = slice(q * width, (q + 1) * width)
        leg_away[:, cut] = jnp.dot(away, leg_v[:, cut], preferred_element_type=F32).astype(BF16)
        leg_copy(q).start()

    here = side_rows(side)
    for q in range(chunks):
        cut = slice(q * width, (q + 1) * width)
        leg_here[0, :, cut] = jnp.dot(here, leg_v[:, cut], preferred_element_type=F32).astype(BF16)

    def below(d, q):
        arrive(2 * (z - d) + core, q)

        @pl.when(z < depth - 1)
        def _():
            to_up(z - d, q).start()

        to_sib(z - d, q).start()

    def above(d, q):
        arrive(2 * (z + d) + core, q)

        @pl.when(z > 0)
        def _():
            to_down(z + d, q).start()

        to_sib(z + d, q).start()

    for d in range(1, depth):
        for q in range(chunks):
            pl.when(z >= d)(functools.partial(below, d, q))
            pl.when(z <= depth - 1 - d)(functools.partial(above, d, q))
    for q in range(chunks):
        leg_copy(q).wait_recv()
    for zz in range(depth):
        for q in range(chunks):
            arrive(2 * zz + 1 - core, q)

    row_pos = split_index(iota((rows_half, span), 0), line)[1]
    same = row_pos == split_index(iota((rows_half, span), 1), cols)[0]
    gather_rows = jnp.where(
        iota((cycles, rows_half), 0) == split_index(iota((cycles, rows_half), 1), line)[0], 1.0, 0.0
    ).astype(BF16)

    def apply(which):
        cross = jnp.zeros((rows_half, span), F32)
        for q in range(chunks):
            cross += lax.dot_general(
                leg_here[which, :, q * width : (q + 1) * width],
                gathered[q].reshape(span, width),
                (((1,), (1,)), ((), ())),
                preferred_element_type=F32,
            )
        own = jnp.where(same, cross, 0.0).astype(BF16)
        return jnp.dot(gather_rows, own, preferred_element_type=F32).astype(BF16)

    harm_copy = pltpu.make_async_remote_copy(
        src_ref=harm_away,
        dst_ref=harm.at[side],
        send_sem=harm_sem.at[0],
        recv_sem=harm_sem.at[1],
        device_id={"mset": partner},
        device_id_type=MESH,
    )
    harm_away[...] = apply(1)
    harm_copy.start()
    harm[side] = apply(0)
    for zz in range(depth):
        for q in range(chunks):
            to_sib(zz, q).wait_send()

            @pl.when((z < depth - 1) & (zz <= z))
            def _():
                to_up(zz, q).wait_send()

            @pl.when((z > 0) & (zz >= z))
            def _():
                to_down(zz, q).wait_send()

    for q in range(chunks):
        leg_copy(q).wait_send()

    row_cycle, _ = split_index(iota((rows_out, cycles), 0), REAL)
    repeat = jnp.where(row_cycle == iota((rows_out, cycles), 1), 1.0, 0.0).astype(BF16)
    row_s = split_index(iota((rows_out, span), 0), REAL)[1]
    col_s = split_index(iota((rows_out, span), 1), REAL)[1]
    keep = row_s == col_s
    src_pos, src_c = split_index(iota((span, 2 * subset), 0), cols)
    src_zz, src_core = split_index(src_pos, 2)
    dst_part, dst_m = split_index(iota((span, 2 * subset), 1), subset)
    same_part = split_index(src_c, REAL)[0] == dst_part
    harm_copy.wait()
    total = jnp.zeros((rows_out, 2 * subset), F32)
    for which in range(2):
        spread = jnp.dot(repeat, harm[which], preferred_element_type=F32)
        picked = jnp.where(keep, spread, 0.0).astype(BF16)
        hit = same_part & (src_zz * group + which * 2 + src_core == dst_m)
        select = jnp.where(hit, 1.0, 0.0).astype(BF16)
        total += jnp.dot(picked, select, preferred_element_type=F32)
    out_ref[...] = total.astype(BF16)


def synthesis_kernel(tiles, scale, m_ref, h_ref, out_ref, h_v, table, buf, sem):
    subset = m_ref.shape[0]
    tile = out_ref.shape[1] // tiles
    load = pltpu.make_async_copy(h_ref, h_v, sem.at[tiles])
    load.start()
    m_col = jnp.zeros((subset, LANES), jnp.int32)
    slot = iota((subset, LANES), 0)
    for i in range(subset):
        m_col = jnp.where(slot == i, m_ref[i], m_col)
    lane = iota((subset, LANES), 1)
    fine = split_index(m_col * lane, NPHI)[1].astype(F32) * (2.0 * math.pi / NPHI)
    coarse = split_index(m_col * (lane * LANES), NPHI)[1].astype(F32) * (2.0 * math.pi / NPHI)
    fine_cos, fine_sin = jnp.cos(fine), jnp.sin(fine)
    coarse_cos, coarse_sin = jnp.cos(coarse), jnp.sin(coarse)

    def fill(t):
        for a in range(t * tile // LANES, (t + 1) * tile // LANES):
            c = coarse_cos[:, a : a + 1]
            s = coarse_sin[:, a : a + 1]
            table[0:subset, a * LANES : (a + 1) * LANES] = (c * fine_cos - s * fine_sin).astype(BF16)
            table[subset : 2 * subset, a * LANES : (a + 1) * LANES] = (
                -(s * fine_cos + c * fine_sin)
            ).astype(BF16)

    copies = []
    fill(0)
    load.wait()
    for t in range(tiles):
        cut = slice(t * tile, (t + 1) * tile)
        total = jnp.dot(h_v[...], table[:, cut], preferred_element_type=F32)
        buf[:, cut] = (total * scale).astype(BF16)
        copies.append(pltpu.make_async_copy(buf.at[:, cut], out_ref.at[:, cut], sem.at[t]))
        copies[-1].start()
        if t + 1 < tiles:
            fill(t + 1)
    for c in copies:
        c.wait()


def body(n, m_list, coeff, blocks, legendre):
    per_device, cols, order_max = coeff.shape
    assert per_device == 1 and n % 4 == 0
    cycles, subset, _ = legendre.shape
    chunks = 3
    depth = n // 4
    rows_in, rows_out = cycles * subset, cycles * REAL
    vmem = pl.BlockSpec(memory_space=pltpu.VMEM)
    hbm = pl.BlockSpec(memory_space=pl.ANY)
    dma = pltpu.SemaphoreType.DMA
    harmonics = pl.pallas_call(
        functools.partial(harmonics_kernel, n, chunks),
        out_shape=jax.ShapeDtypeStruct((rows_out, 2 * subset), BF16),
        in_specs=[pl.BlockSpec(memory_space=pltpu.SMEM), hbm, hbm, hbm],
        out_specs=vmem,
        scratch_shapes=[
            pltpu.VMEM((cols, order_max), BF16),
            pltpu.VMEM((chunks, order_max, order_max // chunks), BF16),
            pltpu.VMEM((rows_in, order_max), BF16),
            pltpu.VMEM((rows_in // 2, order_max), BF16),
            pltpu.VMEM((2, rows_in // 2, order_max), BF16),
            pltpu.VMEM((chunks, n // 2, cols, order_max // chunks), BF16),
            pltpu.VMEM((cycles, n // 2 * cols), BF16),
            pltpu.VMEM((2, cycles, n // 2 * cols), BF16),
            dma((chunks + 2,)),
            dma((chunks, n // 2)),
            dma((chunks, depth)),
            dma((chunks, depth)),
            dma((chunks, depth)),
            dma((chunks,)),
            dma((chunks,)),
            dma((2,)),
        ],
        compiler_params=pltpu.CompilerParams(collective_id=0, has_side_effects=True),
        name="harmonics",
    )(m_list, coeff, blocks, legendre.reshape(rows_in, order_max))
    tiles = 8
    sky = pl.pallas_call(
        functools.partial(synthesis_kernel, tiles, 1.0 / math.sqrt(subset)),
        out_shape=jax.ShapeDtypeStruct((rows_out, NPHI), BF16),
        in_specs=[pl.BlockSpec(memory_space=pltpu.SMEM), hbm],
        out_specs=hbm,
        scratch_shapes=[
            pltpu.VMEM((rows_out, 2 * subset), BF16),
            pltpu.VMEM((2 * subset, NPHI), BF16),
            pltpu.VMEM((rows_out, NPHI), BF16),
            dma((tiles + 1,)),
        ],
        name="synthesis",
    )(m_list, harmonics)
    return sky.reshape(cycles, REAL, NPHI)


def solution(mesh):
    spec = P(("groups", "mset"), None, None)
    return jax.shard_map(
        functools.partial(body, mesh.shape["mset"]),
        mesh=mesh,
        in_specs=(P(), spec, spec, spec),
        out_specs=spec,
        check_vma=False,
    )
```

```python
import functools
import math

import jax
import jax.numpy as jnp
from jax import lax
from jax.experimental import pallas as pl
from jax.experimental.pallas import tpu as pltpu
from jax.sharding import PartitionSpec as P

LL = 3072
REAL = 16
NPHI = 8192
LANES = 128
MESH = pl.DeviceIdType.MESH
F32 = jnp.float32
BF16 = jnp.bfloat16


def iota(shape, dim):
    return lax.broadcasted_iota(jnp.int32, shape, dim)


def split_index(x, size):
    if size & (size - 1) == 0:
        shift = size.bit_length() - 1
        return lax.shift_right_logical(x, jnp.int32(shift)), lax.bitwise_and(x, jnp.int32(size - 1))
    quotient = x // size
    return quotient, x - quotient * size


def harmonics_kernel(
    n, chunks, m_ref, coeff_ref, blocks_ref, leg_ref, out_ref,
    coeff_v, blocks_v, leg_v, leg_away, leg_here, gathered, harm_away, harm,
    load_sem, recv_sem, up_sem, down_sem, sib_sem, leg_send, leg_recv, harm_sem,
):
    subset = m_ref.shape[0]
    cols, order_max = coeff_ref.shape[1], coeff_ref.shape[2]
    width = order_max // chunks
    group = 4
    depth = n // group
    line = 2 * depth
    rows_in = leg_ref.shape[0]
    rows_out = out_ref.shape[0]
    cycles = rows_in // subset
    rows_half = cycles * line
    span = line * cols
    me = lax.axis_index("mset")
    core = lax.rem(me, 2)
    side = lax.rem(lax.div(me, 2), 2)
    z = lax.div(me, group)
    sibling = me + 1 - 2 * core
    partner = me + 2 - 4 * side

    def load_block(q):
        return pltpu.make_async_copy(
            blocks_ref.at[0, :, pl.ds(q * width, width)], blocks_v.at[q], load_sem.at[q]
        )

    coeff_load = pltpu.make_async_copy(coeff_ref.at[0], coeff_v, load_sem.at[chunks])
    leg_load = pltpu.make_async_copy(leg_ref, leg_v, load_sem.at[chunks + 1])
    coeff_load.start()
    for q in range(chunks):
        load_block(q).start()
    leg_load.start()

    barrier = pltpu.get_barrier_semaphore()

    def greet(target):
        pl.semaphore_signal(barrier, inc=1, device_id={"mset": target}, device_id_type=MESH)

    greet(sibling)
    greet(partner)

    @pl.when(z > 0)
    def _():
        greet(me - group)

    @pl.when(z < depth - 1)
    def _():
        greet(me + group)

    def piece(pos, q):
        return gathered.at[q, pos]

    def copy(pos, q, target, send_sem):
        return pltpu.make_async_remote_copy(
            src_ref=piece(pos, q),
            dst_ref=piece(pos, q),
            send_sem=send_sem,
            recv_sem=recv_sem.at[q, pos],
            device_id={"mset": target},
            device_id_type=MESH,
        )

    def to_up(zz, q):
        return copy(2 * zz + core, q, me + group, up_sem.at[q, zz])

    def to_down(zz, q):
        return copy(2 * zz + core, q, me - group, down_sem.at[q, zz])

    def to_sib(zz, q):
        return copy(2 * zz + core, q, sibling, sib_sem.at[q, zz])

    def arrive(pos, q):
        copy(pos, q, sibling, sib_sem.at[q, 0]).wait_recv()

    def leg_copy(q):
        return pltpu.make_async_remote_copy(
            src_ref=leg_away.at[:, pl.ds(q * width, width)],
            dst_ref=leg_here.at[1, :, pl.ds(q * width, width)],
            send_sem=leg_send.at[q],
            recv_sem=leg_recv.at[q],
            device_id={"mset": partner},
            device_id_type=MESH,
        )

    def side_rows(which):
        row_cycle, row_pos = split_index(iota((rows_half, rows_in), 0), line)
        row_zz, row_core = split_index(row_pos, 2)
        wanted = row_cycle * subset + row_zz * group + which * 2 + row_core
        return jnp.where(iota((rows_half, rows_in), 1) == wanted, 1.0, 0.0).astype(BF16)

    order = LL - m_ref[me]
    coeff_load.wait()
    masked = jnp.where(iota((cols, order_max), 1) < order, coeff_v[...].astype(F32), 0.0).astype(BF16)
    for q in range(chunks):
        load_block(q).wait()
        product = jnp.dot(masked, blocks_v[q], preferred_element_type=F32)
        valid = iota((cols, width), 1) + q * width < order
        gathered[q, 2 * z + core] = jnp.where(valid, product, 0.0).astype(BF16)

        if q == 0:
            peers = 2 + jnp.where(z > 0, 1, 0) + jnp.where(z < depth - 1, 1, 0)
            pl.semaphore_wait(barrier, peers)

        @pl.when(z < depth - 1)
        def _():
            to_up(z, q).start()

        @pl.when(z > 0)
        def _():
            to_down(z, q).start()

        to_sib(z, q).start()

    away = side_rows(1 - side)
    leg_load.wait()
    for q in range(chunks):
        cut = slice(q * width, (q + 1) * width)
        leg_away[:, cut] = jnp.dot(away, leg_v[:, cut], preferred_element_type=F32).astype(BF16)
        leg_copy(q).start()

    here = side_rows(side)
    for q in range(chunks):
        cut = slice(q * width, (q + 1) * width)
        leg_here[0, :, cut] = jnp.dot(here, leg_v[:, cut], preferred_element_type=F32).astype(BF16)

    def below(d, q):
        arrive(2 * (z - d) + core, q)

        @pl.when(z < depth - 1)
        def _():
            to_up(z - d, q).start()

        to_sib(z - d, q).start()

    def above(d, q):
        arrive(2 * (z + d) + core, q)

        @pl.when(z > 0)
        def _():
            to_down(z + d, q).start()

        to_sib(z + d, q).start()

    for d in range(1, depth):
        for q in range(chunks):
            pl.when(z >= d)(functools.partial(below, d, q))
            pl.when(z <= depth - 1 - d)(functools.partial(above, d, q))
    for q in range(chunks):
        leg_copy(q).wait_recv()
    for zz in range(depth):
        for q in range(chunks):
            arrive(2 * zz + 1 - core, q)

    row_pos = split_index(iota((rows_half, span), 0), line)[1]
    same = row_pos == split_index(iota((rows_half, span), 1), cols)[0]
    gather_rows = jnp.where(
        iota((cycles, rows_half), 0) == split_index(iota((cycles, rows_half), 1), line)[0], 1.0, 0.0
    ).astype(BF16)

    def apply(which):
        cross = jnp.zeros((rows_half, span), F32)
        for q in range(chunks):
            cross += lax.dot_general(
                leg_here[which, :, q * width : (q + 1) * width],
                gathered[q].reshape(span, width),
                (((1,), (1,)), ((), ())),
                preferred_element_type=F32,
            )
        own = jnp.where(same, cross, 0.0).astype(BF16)
        return jnp.dot(gather_rows, own, preferred_element_type=F32).astype(BF16)

    harm_copy = pltpu.make_async_remote_copy(
        src_ref=harm_away,
        dst_ref=harm.at[side],
        send_sem=harm_sem.at[0],
        recv_sem=harm_sem.at[1],
        device_id={"mset": partner},
        device_id_type=MESH,
    )
    harm_away[...] = apply(1)
    harm_copy.start()
    harm[side] = apply(0)
    for zz in range(depth):
        for q in range(chunks):
            to_sib(zz, q).wait_send()

            @pl.when((z < depth - 1) & (zz <= z))
            def _():
                to_up(zz, q).wait_send()

            @pl.when((z > 0) & (zz >= z))
            def _():
                to_down(zz, q).wait_send()

    for q in range(chunks):
        leg_copy(q).wait_send()

    row_cycle, _ = split_index(iota((rows_out, cycles), 0), REAL)
    repeat = jnp.where(row_cycle == iota((rows_out, cycles), 1), 1.0, 0.0).astype(BF16)
    row_s = split_index(iota((rows_out, span), 0), REAL)[1]
    col_s = split_index(iota((rows_out, span), 1), REAL)[1]
    keep = row_s == col_s
    src_pos, src_c = split_index(iota((span, 2 * subset), 0), cols)
    src_zz, src_core = split_index(src_pos, 2)
    dst_part, dst_m = split_index(iota((span, 2 * subset), 1), subset)
    same_part = split_index(src_c, REAL)[0] == dst_part
    harm_copy.wait()
    total = jnp.zeros((rows_out, 2 * subset), F32)
    for which in range(2):
        spread = jnp.dot(repeat, harm[which], preferred_element_type=F32)
        picked = jnp.where(keep, spread, 0.0).astype(BF16)
        hit = same_part & (src_zz * group + which * 2 + src_core == dst_m)
        select = jnp.where(hit, 1.0, 0.0).astype(BF16)
        total += jnp.dot(picked, select, preferred_element_type=F32)
    out_ref[...] = total.astype(BF16)


def synthesis_kernel(tiles, scale, m_ref, h_v, out_ref, table, buf, sem):
    subset = m_ref.shape[0]
    tile = out_ref.shape[1] // tiles
    m_col = jnp.zeros((subset, LANES), jnp.int32)
    slot = iota((subset, LANES), 0)
    for i in range(subset):
        m_col = jnp.where(slot == i, m_ref[i], m_col)
    lane = iota((subset, LANES), 1)
    fine = split_index(m_col * lane, NPHI)[1].astype(F32) * (2.0 * math.pi / NPHI)
    coarse = split_index(m_col * (lane * LANES), NPHI)[1].astype(F32) * (2.0 * math.pi / NPHI)
    fine_cos, fine_sin = jnp.cos(fine), jnp.sin(fine)
    coarse_cos, coarse_sin = jnp.cos(coarse), jnp.sin(coarse)

    def fill(t):
        for a in range(t * tile // LANES, (t + 1) * tile // LANES):
            c = coarse_cos[:, a : a + 1]
            s = coarse_sin[:, a : a + 1]
            table[0:subset, a * LANES : (a + 1) * LANES] = (c * fine_cos - s * fine_sin).astype(BF16)
            table[subset : 2 * subset, a * LANES : (a + 1) * LANES] = (
                -(s * fine_cos + c * fine_sin)
            ).astype(BF16)

    copies = []
    fill(0)
    for t in range(tiles):
        cut = slice(t * tile, (t + 1) * tile)
        total = jnp.dot(h_v[...], table[:, cut], preferred_element_type=F32)
        buf[:, cut] = (total * scale).astype(BF16)
        copies.append(pltpu.make_async_copy(buf.at[:, cut], out_ref.at[:, cut], sem.at[t]))
        copies[-1].start()
        if t + 1 < tiles:
            fill(t + 1)
    for c in copies:
        c.wait()


def body(n, m_list, coeff, blocks, legendre):
    per_device, cols, order_max = coeff.shape
    assert per_device == 1 and n % 4 == 0
    cycles, subset, _ = legendre.shape
    chunks = 3
    depth = n // 4
    rows_in, rows_out = cycles * subset, cycles * REAL
    keep = functools.partial(pltpu.with_memory_space_constraint, memory_space=pltpu.HBM)
    vmem = pl.BlockSpec(memory_space=pltpu.VMEM)
    hbm = pl.BlockSpec(memory_space=pltpu.HBM)
    dma = pltpu.SemaphoreType.DMA
    harmonics = pl.pallas_call(
        functools.partial(harmonics_kernel, n, chunks),
        out_shape=jax.ShapeDtypeStruct((rows_out, 2 * subset), BF16),
        in_specs=[pl.BlockSpec(memory_space=pltpu.SMEM), hbm, hbm, hbm],
        out_specs=vmem,
        scratch_shapes=[
            pltpu.VMEM((cols, order_max), BF16),
            pltpu.VMEM((chunks, order_max, order_max // chunks), BF16),
            pltpu.VMEM((rows_in, order_max), BF16),
            pltpu.VMEM((rows_in // 2, order_max), BF16),
            pltpu.VMEM((2, rows_in // 2, order_max), BF16),
            pltpu.VMEM((chunks, n // 2, cols, order_max // chunks), BF16),
            pltpu.VMEM((cycles, n // 2 * cols), BF16),
            pltpu.VMEM((2, cycles, n // 2 * cols), BF16),
            dma((chunks + 2,)),
            dma((chunks, n // 2)),
            dma((chunks, depth)),
            dma((chunks, depth)),
            dma((chunks, depth)),
            dma((chunks,)),
            dma((chunks,)),
            dma((2,)),
        ],
        compiler_params=pltpu.CompilerParams(collective_id=0, has_side_effects=True, vmem_limit_bytes=40 << 20),
        name="harmonics",
    )(m_list, keep(coeff), keep(blocks), keep(legendre.reshape(rows_in, order_max)))
    tiles = 8
    sky = pl.pallas_call(
        functools.partial(synthesis_kernel, tiles, 1.0 / math.sqrt(subset)),
        out_shape=jax.ShapeDtypeStruct((rows_out, NPHI), BF16),
        in_specs=[pl.BlockSpec(memory_space=pltpu.SMEM), vmem],
        out_specs=hbm,
        scratch_shapes=[
            pltpu.VMEM((2 * subset, NPHI), BF16),
            pltpu.VMEM((rows_out, NPHI), BF16),
            dma((tiles,)),
        ],
        name="synthesis", compiler_params=pltpu.CompilerParams(vmem_limit_bytes=40 << 20),
    )(m_list, harmonics)
    return sky.reshape(cycles, REAL, NPHI)


def solution(mesh):
    spec = P(("groups", "mset"), None, None)
    return jax.shard_map(
        functools.partial(body, mesh.shape["mset"]),
        mesh=mesh,
        in_specs=(P(), spec, spec, spec),
        out_specs=spec,
        check_vma=False,
    )
```
